32 devices in a mesh: fsdp: 2 (over y), ctx: 8 (over z, x), tp: 2 (over core).
Axes of the slice: x: 2, y: 2, z: 4, core: 2. Of those that a mesh axis runs over, the one named last changes fastest.
Arguments:
- hidden_in: bfloat16 [2, 2048, 1024], P('fsdp', 'ctx'), may hold values from -6 to 6
- segments: int32 [2, 2048], P('fsdp', 'ctx'), may hold values from 0 to 2, never falling along the last dimension, each value on 1 to 1024 neighbouring positions
- cotangent: bfloat16 [2, 2048, 1024], P('fsdp', 'ctx'), may hold values from -6 to 6
- norm_gain: float32 [2, 1024], P('fsdp'), may hold values from 0.5 to 1.5
- in_proj: bfloat16 [2, 1024, 2, 2048], P(None, ('fsdp', 'ctx'), None, 'tp'), may hold values from -0.1875 to 0.1875
- step_proj: bfloat16 [2, 1024, 32], P(None, ('fsdp', 'ctx'), 'tp'), may hold values from -0.1875 to 0.1875
- state_proj: bfloat16 [2, 1024, 256], P(None, ('fsdp', 'ctx')), may hold values from -0.1875 to 0.1875
- out_proj: bfloat16 [2, 1024, 2048], P(None, ('fsdp', 'ctx'), 'tp'), may hold values from -0.125 to 0.125
- conv_inner: float32 [2, 4, 2048], P('fsdp', None, 'tp'), may hold values from -3 to 3
- inner_bias: float32 [2, 2048], P('fsdp', 'tp'), may hold values from -0.5 to 0.5
- conv_state: float32 [2, 4, 256], P('fsdp'), may hold values from -3 to 3
- state_bias: float32 [2, 256], P('fsdp'), may hold values from -0.5 to 0.5
- step_bias: float32 [2, 32], P('fsdp', 'tp'), may hold values from -5 to 0
- decay_log: float32 [2, 32], P('fsdp', 'tp'), may hold values from -6.9 to -1.9
- skip_scale: float32 [2, 32], P('fsdp', 'tp'), may hold values from 0.5 to 2
- gate_gain: float32 [2, 2048], P('fsdp', 'tp'), may hold values from 0.5 to 1.5
Outputs:
- hidden_out: bfloat16 [2, 2048, 1024], P('fsdp', 'ctx')
- hidden_grad: float32 [2, 2048, 1024], P('fsdp', 'ctx')
- grad_norm_gain: float32 [2, 1024], P('fsdp')
- grad_in_proj: float32 [2, 1024, 2, 2048], P(None, ('fsdp', 'ctx'), None, 'tp')
- grad_step_proj: float32 [2, 1024, 32], P(None, ('fsdp', 'ctx'), 'tp')
- grad_state_proj: float32 [2, 1024, 256], P(None, ('fsdp', 'ctx'))
- grad_out_proj: float32 [2, 1024, 2048], P(None, ('fsdp', 'ctx'), 'tp')
- grad_conv_inner: float32 [2, 4, 2048], P('fsdp', None, 'tp')
- grad_inner_bias: float32 [2, 2048], P('fsdp', 'tp')
- grad_conv_state: float32 [2, 4, 256], P('fsdp')
- grad_state_bias: float32 [2, 256], P('fsdp')
- grad_step_bias: float32 [2, 32], P('fsdp', 'tp')
- grad_decay_log: float32 [2, 32], P('fsdp', 'tp')
- grad_skip_scale: float32 [2, 32], P('fsdp', 'tp')
- grad_gate_gain: float32 [2, 2048], P('fsdp', 'tp')
The draws below stay inside these ranges and needn't reach their ends.
Inputs may be any that keep to these rules, and one draw needn't show every extreme that they name: `segments`: in each row the segment numbers start at 0, never fall and take every value up to 2; one packed sequence has exactly 1024 positions and none has more.
All inputs are finite; a program needn't handle non-finite values.
Results may differ from the reference program's by a relative error of at most 0.02.
The reference program's roundings to bfloat16 on the way (of `normed`, `branch` and `outward`) count: a program that leaves them out, or rounds other values in their place, can miss the bound.
Values may be sent and summed in bfloat16 or wider, within the bound.
No kernel may reach another device: no remote copies, remote signals or barrier semaphores. Data moves between devices by JAX's collectives and lax.ppermute only.
A program may use at most 320 MiB of HBM per device.

```python
import math
import jax
import jax.numpy as jnp
import numpy as np
from jax import lax

D = 1024
INNER = 2048
HEADS = 32
STATE = 128
CONV = 4
BLOCK = 64
LAYERS = 2
SEGS = 3
ROWS = 2
SEQ = 2048
SEG_MOST = 1024


def levels(key, shape, cuts, least, top_value):
    level = 1.0
    for axis_at, shards_of in cuts:
        draws = jax.random.uniform(jax.random.fold_in(jax.random.fold_in(key, 6), axis_at), (shards_of,), jnp.float32, least / len(cuts), top_value / len(cuts))
        level = level * jnp.repeat(jnp.exp(draws), shape[axis_at] // shards_of).reshape((-1,) + (1,) * (len(shape) - 1 - axis_at))
    return level


def split_up(amount, total, limit, lean):
    loads = [(1 << 20) // math.isqrt(standing ** lean) + 1 for standing in range(2, amount + 1)]
    surplus, counts = total - limit - (amount - 1), [1] * (amount - 1)
    while surplus > 0:
        free = [i for i in range(amount - 1) if counts[i] < limit]
        whole, left = sum([loads[i] for i in free]), surplus
        for i in free:
            addition = min(limit - counts[i], max(1, left * loads[i] // whole), surplus)
            counts[i] = counts[i] + addition
            surplus = surplus - addition
    return np.array([limit] + counts)


def uneven_parts(stream_key, number_of, total, bound, skew):
    if number_of == 2:
        one = jax.random.randint(stream_key, (), max(1, total - bound), min(bound, total - 1) + 1)
        return jnp.stack([one, total - one])
    sizes = jnp.asarray(split_up(number_of, total, bound, skew), jnp.int32)
    pairs = (number_of - 1) // 2
    donor, receiver = sizes[1:1 + 2 * pairs:2], sizes[2:2 + 2 * pairs:2]
    room = jnp.minimum(donor - 1, bound - receiver)
    moved = jax.random.randint(jax.random.fold_in(stream_key, 1), (pairs,), 0, 1 << 20) % (room + 1)
    sizes = sizes.at[1:1 + 2 * pairs:2].set(donor - moved).at[2:2 + 2 * pairs:2].set(receiver + moved)
    return sizes[jax.random.permutation(jax.random.fold_in(stream_key, 2), number_of)]


def scatter_about(rng, dims, width, bound, cuts=(), kind=jnp.bfloat16):
    array = width * jax.random.normal(rng, dims, jnp.float32)
    if cuts:
        array = array * levels(rng, dims, cuts, -0.22, 0.18)
    return jnp.clip(array, -bound, bound).astype(kind)


def setup_inputs(seed: int = 0) -> dict:
    seeds = jax.random.split(jax.random.key(seed), 17)
    return {
        "hidden_in": scatter_about(seeds[0], (ROWS, SEQ, D), 1.0, 6.0, ((0, 2), (1, 8))),
        "segments": jax.vmap(lambda own: jnp.searchsorted(jnp.cumsum(uneven_parts(own, SEGS, SEQ, SEG_MOST, 0)), jnp.arange(SEQ), side="right"))(jax.random.split(seeds[1], ROWS)).reshape((ROWS, SEQ)).astype(jnp.int32),
        "cotangent": scatter_about(seeds[2], (ROWS, SEQ, D), 1.0, 6.0, ((0, 2), (1, 8))),
        "norm_gain": jnp.clip(1.0 + 0.1 * jax.random.normal(seeds[3], (LAYERS, D), jnp.float32), 0.5, 1.5),
        "in_proj": scatter_about(seeds[4], (LAYERS, D, 2, INNER), D ** -0.5, 0.1875, ((1, 16), (3, 2))),
        "step_proj": scatter_about(seeds[5], (LAYERS, D, HEADS), D ** -0.5, 0.1875, ((1, 16), (2, 2))),
        "state_proj": scatter_about(seeds[6], (LAYERS, D, 2 * STATE), D ** -0.5, 0.1875, ((1, 16),)),
        "out_proj": scatter_about(seeds[7], (LAYERS, D, INNER), INNER ** -0.5, 0.125, ((1, 16), (2, 2))),
        "conv_inner": scatter_about(seeds[8], (LAYERS, CONV, INNER), CONV ** -0.5, 3.0, ((0, 2), (2, 2)), jnp.float32),
        "inner_bias": jnp.clip(jax.random.uniform(seeds[9], (LAYERS, INNER), jnp.float32, -0.5, 0.5) * levels(seeds[9], (LAYERS, INNER), ((0, 2), (1, 2)), -0.4, 0.0), -0.5, 0.5),
        "conv_state": scatter_about(seeds[10], (LAYERS, CONV, 2 * STATE), CONV ** -0.5, 3.0, ((0, 2),), jnp.float32),
        "state_bias": jnp.clip(jax.random.uniform(seeds[11], (LAYERS, 2 * STATE), jnp.float32, -0.5, 0.5) * levels(seeds[11], (LAYERS, 2 * STATE), ((0, 2),), -0.4, 0.0), -0.5, 0.5),
        "step_bias": jnp.clip(-5.0 + 5.0 * jax.random.uniform(seeds[12], (LAYERS, HEADS), jnp.float32) ** levels(seeds[12], (LAYERS, HEADS), ((0, 2), (1, 2)), -0.2, 0.2), -5.0, 0.0),
        "decay_log": jnp.clip(-6.9 + 5 * jax.random.uniform(seeds[13], (LAYERS, HEADS), jnp.float32) ** levels(seeds[13], (LAYERS, HEADS), ((0, 2), (1, 2)), -0.2, 0.2), -6.9, -1.9),
        "skip_scale": jnp.clip(0.5 + 1.5 * jax.random.uniform(seeds[14], (LAYERS, HEADS), jnp.float32) ** levels(seeds[14], (LAYERS, HEADS), ((0, 2), (1, 2)), -0.2, 0.2), 0.5, 2.0),
        "gate_gain": jnp.clip(1.0 + 0.1 * jax.random.normal(seeds[15], (LAYERS, INNER), jnp.float32), 0.5, 1.5),
    }


EPSILON = 1e-05
HIGHEST = lax.Precision.HIGHEST

def matmul(former, latter):
    return jnp.dot(former, latter, preferred_element_type=jnp.float32)

def matmul_tn(former, latter):
    return lax.dot_general(former, latter, (((0,), (0,)), ((), ())), preferred_element_type=jnp.float32)

def matmul_nt(former, latter):
    return lax.dot_general(former, latter, (((1,), (1,)), ((), ())), preferred_element_type=jnp.float32)

def rms_norm(residual, scaling):
    return residual * lax.rsqrt(lax.optimization_barrier(jnp.mean(residual * residual, axis=1, keepdims=True)) + EPSILON) * scaling[None, :]

def causal_conv(padded, labels, kernel, offset):
    length = padded.shape[0] - kernel.shape[0] + 1
    current = labels[kernel.shape[0] - 1:]
    result = jnp.zeros((length, padded.shape[1]), jnp.float32) + offset[None, :]
    for lag_index in range(kernel.shape[0]):
        matched = (labels[lag_index:lag_index + length] == current).astype(jnp.float32)
        result = result + kernel[lag_index][None, :] * padded[lag_index:lag_index + length] * matched[:, None]
    return result

def block_terms(values, write_map, read_map, step_size, decay_rate, labels, before):
    logdecay = step_size * decay_rate[None, :]
    cumulative = jnp.cumsum(logdecay, axis=0)
    position = jnp.arange(values.shape[0])
    visible = (position[:, None] >= position[None, :]) & (labels[:, None] == labels[None, :])
    spread = cumulative[:, None, :] - cumulative[None, :, :]
    kernels = jnp.exp(jnp.where(visible[:, :, None], spread, -1e+30))
    affinity = jnp.dot(read_map, write_map.T, precision=HIGHEST)
    weights = affinity[:, :, None] * kernels * step_size[None, :, :]
    within = jnp.einsum('tsh,shp->thp', weights, values, precision=HIGHEST)
    closing = labels[-1]
    ending = jnp.exp(cumulative[-1][None, :] - cumulative) * (labels == closing).astype(jnp.float32)[:, None] * step_size
    produced = jnp.einsum('sh,shp,sn->hpn', ending, values, write_map, precision=HIGHEST)
    inflow = jnp.exp(cumulative) * (labels == before).astype(jnp.float32)[:, None]
    passing = jnp.exp(cumulative[-1]) * (closing == before).astype(jnp.float32)
    return (within, produced, inflow, passing)

def mixer_branch(gate_pre, inner_pre, step_pre, state_pre, kernel, offset, step_bias, decay_log, skip_scale, gate_gain, labels):
    tokens = gate_pre.shape[0]
    inner_width = gate_pre.shape[1]
    head_count = step_pre.shape[1]
    head_size = inner_width // head_count
    state_size = state_pre.shape[1] // 2
    margin = kernel.shape[0] - 1
    joined = jnp.concatenate([inner_pre, state_pre], axis=1)
    padded = jnp.concatenate([jnp.zeros((margin, joined.shape[1]), jnp.float32), joined], axis=0)
    padded_labels = jnp.concatenate([jnp.zeros((margin,), jnp.int32), labels], axis=0)
    active = jax.nn.silu(causal_conv(padded, padded_labels, kernel, offset))
    values = active[:, :inner_width].reshape(tokens, head_count, head_size)
    write_map = active[:, inner_width:inner_width + state_size]
    read_map = active[:, inner_width + state_size:]
    step_size = jax.nn.softplus(step_pre + step_bias[None, :])
    decay_rate = -jnp.exp(decay_log)
    blocks = tokens // BLOCK

    def advance(carried_in, pieces):
        memory, before = carried_in
        part_values, part_write, part_read, part_step, part_labels = pieces
        within, produced, inflow, passing = block_terms(part_values, part_write, part_read, part_step, decay_rate, part_labels, before)
        carried = inflow[:, :, None] * jnp.einsum('tn,hpn->thp', part_read, memory, precision=HIGHEST)
        output = within + carried + skip_scale[None, :, None] * part_values
        return ((passing[:, None, None] * memory + produced, part_labels[-1]), output)
    initial = (jnp.zeros((head_count, head_size, state_size), jnp.float32), jnp.zeros((), jnp.int32))
    blocked = (values.reshape(blocks, BLOCK, head_count, head_size), write_map.reshape(blocks, BLOCK, state_size), read_map.reshape(blocks, BLOCK, state_size), step_size.reshape(blocks, BLOCK, head_count), labels.reshape(blocks, BLOCK))
    _, outputs = lax.scan(jax.checkpoint(advance), initial, blocked)
    mixed_all = outputs.reshape(tokens, inner_width)
    gated_rows = mixed_all * jax.nn.silu(gate_pre)
    return gated_rows * lax.rsqrt(lax.optimization_barrier(jnp.mean(gated_rows * gated_rows, axis=1, keepdims=True)) + EPSILON) * gate_gain[None, :]

def layer_parts(residual, params):
    prenorm, weight_in, weight_step, weight_state = params[:4]
    model_width = residual.shape[1]
    normed = rms_norm(residual, prenorm).astype(jnp.bfloat16)
    inner_width = weight_in.shape[2]
    projected = matmul(normed, weight_in.reshape(model_width, 2 * inner_width))
    inputs = (projected[:, :inner_width], projected[:, inner_width:], matmul(normed, weight_step), matmul(normed, weight_state))
    return (normed, inputs)

def layer_forward(residual, labels, params):
    normed, inputs = layer_parts(residual, params)
    branch = mixer_branch(*inputs, *params[5:], labels).astype(jnp.bfloat16)
    return residual + matmul_nt(branch, params[4])

def layer_backward(residual, labels, params, upstream):
    prenorm, weight_in, weight_step, weight_state, weight_out = params[:5]
    model_width = residual.shape[1]
    normed, inputs = layer_parts(residual, params)

    def local_branch(*floats):
        return mixer_branch(*floats, labels)
    branch, branch_pull = jax.vjp(local_branch, *inputs, *params[5:])
    rounded = branch.astype(jnp.bfloat16)
    outward = upstream.astype(jnp.bfloat16)
    grad_out = matmul_tn(outward, rounded)
    grad_branch = matmul(outward, weight_out)
    pulled = branch_pull(grad_branch)
    grad_pre = jnp.concatenate([pulled[0], pulled[1]], axis=1).astype(jnp.bfloat16)
    grad_step = pulled[2].astype(jnp.bfloat16)
    grad_state = pulled[3].astype(jnp.bfloat16)
    grad_in = matmul_tn(normed, grad_pre).reshape(weight_in.shape)
    grad_step_proj = matmul_tn(normed, grad_step)
    grad_state_proj = matmul_tn(normed, grad_state)
    grad_normed = matmul_nt(grad_pre, weight_in.reshape(model_width, -1)) + matmul_nt(grad_step, weight_step) + matmul_nt(grad_state, weight_state)
    _, norm_pull = jax.vjp(rms_norm, residual, prenorm)
    grad_residual, grad_prenorm = norm_pull(grad_normed)
    return (upstream + grad_residual, (grad_prenorm, grad_in, grad_step_proj, grad_state_proj, grad_out) + tuple(pulled[4:]))

def reference(hidden_in, segments, cotangent, norm_gain, in_proj, step_proj, state_proj, out_proj, conv_inner, inner_bias, conv_state, state_bias, step_bias, decay_log, skip_scale, gate_gain):
    layered = tuple(((norm_gain[ordinal], in_proj[ordinal], step_proj[ordinal], state_proj[ordinal], out_proj[ordinal], jnp.concatenate([conv_inner[ordinal], conv_state[ordinal]], axis=1), jnp.concatenate([inner_bias[ordinal], state_bias[ordinal]], axis=0), step_bias[ordinal], decay_log[ordinal], skip_scale[ordinal], gate_gain[ordinal]) for ordinal in range(LAYERS)))

    def one_row(totals, row_data):
        residual_row, labels, upstream = row_data
        residuals = [residual_row.astype(jnp.float32)]
        for ordinal in range(LAYERS):
            residuals.append(layer_forward(residuals[ordinal], labels, layered[ordinal]))
        flowing = upstream.astype(jnp.float32)
        updated = list(totals)
        for ordinal in reversed(range(LAYERS)):
            flowing, layer_grads = layer_backward(residuals[ordinal], labels, layered[ordinal], flowing)
            updated[ordinal] = jax.tree.map(jnp.add, updated[ordinal], layer_grads)
        return (tuple(updated), (residuals[LAYERS].astype(jnp.bfloat16), flowing))
    starting_totals = jax.tree.map(lambda leaf_array: jnp.zeros(leaf_array.shape, jnp.float32), layered)
    totals, (hidden_out, hidden_grad) = lax.scan(one_row, starting_totals, (hidden_in, segments, cotangent))

    def stacked(member):
        return jnp.stack([totals[ordinal][member] for ordinal in range(LAYERS)], axis=0)
    kernels_all = stacked(5)
    offsets_all = stacked(6)
    return (hidden_out, hidden_grad, stacked(0), stacked(1), stacked(2), stacked(3), stacked(4), kernels_all[:, :, :INNER], offsets_all[:, :INNER], kernels_all[:, :, INNER:], offsets_all[:, INNER:], stacked(7), stacked(8), stacked(9), stacked(10))
```

```python
import functools

import jax
import jax.numpy as jnp
from jax import lax
from jax.experimental import pallas as pl
from jax.experimental.pallas import tpu as pltpu
from jax.sharding import PartitionSpec as P

EPSILON = 1e-05
HIGHEST = lax.Precision.HIGHEST
LANES = 128
HALO = 8
ROWS = ("fsdp", "ctx")
HIDE = -1e30
F32 = jnp.float32
BF16 = jnp.bfloat16

INFLOW, CLOSING, AHEAD = 8, 9, 16
BIAS, DECAY, SKIP = 0, 1, 2


def shifted(block, axis, distance):
    devices = range(lax.axis_size(axis))
    route = [(i - distance, i) for i in devices if i - distance in devices]
    return lax.ppermute(block, axis, route)


def swapped(block, axis):
    count = lax.axis_size(axis)
    return lax.ppermute(block, axis, [(i, (i + 1) % count) for i in range(count)])


def pair_sum(block, axis):
    total, moving = (block.astype(F32), block)
    for _ in range(lax.axis_size(axis) - 1):
        moving = swapped(moving, axis)
        total = total + moving.astype(F32)
    return total


def mm(a, b, ca, cb):
    return lax.dot_general(a, b, (((ca,), (cb,)), ((), ())), preferred_element_type=F32)


def fine(a, b, ca, cb):
    return lax.dot_general(
        a, b, (((ca,), (cb,)), ((), ())), precision=HIGHEST, preferred_element_type=F32
    )


def sigmoid(v):
    return 1.0 / (1.0 + jnp.exp(-v))


def lower_ones(length):
    row = lax.broadcasted_iota(jnp.int32, (length, length), 0)
    col = lax.broadcasted_iota(jnp.int32, (length, length), 1)
    return (row >= col).astype(F32)


def spread(table, tile, size):
    per = LANES // size
    lane = lax.broadcasted_iota(jnp.int32, (table.shape[0], LANES), 1)
    first = tile * per
    out = jnp.broadcast_to(table[:, first : first + 1], lane.shape)
    for k in range(1, per):
        column = jnp.broadcast_to(table[:, first + k : first + k + 1], lane.shape)
        out = jnp.where(lane >= k * size, column, out)
    return out


def head_columns(tile, size):
    row = lax.broadcasted_iota(jnp.int32, (LANES, LANES), 0)
    col = lax.broadcasted_iota(jnp.int32, (LANES, LANES), 1)
    return (row // size + tile * (LANES // size) == col).astype(F32)


def tiles_of(width):
    return [(j, slice(j * LANES, (j + 1) * LANES)) for j in range(width // LANES)]


def step_sizes(pre, bias):
    v = pre + bias
    return jnp.maximum(v, 0.0) + jnp.log1p(jnp.exp(-jnp.abs(v)))


def front_kernel(dims, proj, where_, taps, heads, z, act, xs, step, cum, closing):
    tokens, inner, state, lags, size = dims
    for _, cols in tiles_of(inner + 2 * state):
        source = slice(inner + cols.start, inner + cols.stop)
        total = jnp.broadcast_to(taps[lags : lags + 1, cols], (tokens, LANES))
        for k in range(lags):
            begin = HALO - lags + 1 + k
            piece = taps[k : k + 1, cols] * proj[begin : begin + tokens, source]
            if k < lags - 1:
                piece = piece * where_[:, k : k + 1]
            total = total + piece
        z[:, cols] = total
        act[:, cols] = total * sigmoid(total)
    steps = step_sizes(proj[HALO:, 2 * inner + 2 * state :], heads[BIAS : BIAS + 1, :])
    rate = -jnp.exp(heads[DECAY : DECAY + 1, :])
    summed = fine(lower_ones(tokens), steps * rate, 1, 0)
    step[...] = steps
    cum[...] = summed
    ending = jnp.exp(summed[tokens - 1 :, :] - summed) * where_[:, CLOSING : CLOSING + 1]
    write = act[:, inner : inner + state]
    for j, cols in tiles_of(inner):
        scaled = act[:, cols] * spread(steps, j, size)
        xs[:, cols] = scaled
        closing[cols, :] = fine(scaled * spread(ending, j, size), write, 0, 0)


def within_kernel(dims, act, xs, cum, hide, heads, within):
    tokens, inner, state, lags, size = dims
    write, read = (act[:, inner : inner + state], act[:, inner + state :])
    scores = fine(read, write, 1, 1)
    sums = cum[...]
    sums_t = sums.T
    hidden = hide[...]
    lane = lax.broadcasted_iota(jnp.int32, (tokens, LANES), 1)
    per = LANES // size
    for j, cols in tiles_of(inner):
        x = xs[:, cols]
        out = None
        for k in range(per):
            h = j * per + k
            decay = jnp.exp(sums[:, h : h + 1] - sums_t[h : h + 1, :] + hidden)
            y = fine(scores * decay, x, 1, 0)
            out = y if k == 0 else jnp.where(lane >= k * size, y, out)
        within[:, cols] = out + spread(heads[SKIP : SKIP + 1, :], j, size) * act[:, cols]


def join_kernel(dims, within, act, incoming, cum, where_, gate, mixed, gated, squares):
    tokens, inner, state, lags, size = dims
    read = act[:, inner + state :]
    inflow = jnp.exp(cum[...]) * where_[:, INFLOW : INFLOW + 1]
    total = jnp.zeros((tokens, LANES), F32)
    for j, cols in tiles_of(inner):
        reached = fine(read, incoming[cols, :], 1, 1)
        m = within[:, cols] + spread(inflow, j, size) * reached
        g = gate[HALO:, cols]
        v = m * (g * sigmoid(g))
        mixed[:, cols] = m
        gated[:, cols] = v
        total = total + v * v
    squares[...] = fine(jnp.ones((8, LANES), F32), total, 1, 1)


def gate_back_kernel(
    dims, pulled, gated, mixed, gate, factors, gain, act, cum, where_, dy, dgate, carried, dgain
):
    tokens, inner, state, lags, size = dims
    scale, other = (factors[:, 0:1], factors[:, 1:2])
    read = act[:, inner + state :]
    inflow = jnp.exp(cum[...]) * where_[:, INFLOW : INFLOW + 1]
    for j, cols in tiles_of(inner):
        b = pulled[:, cols]
        v = gated[:, cols]
        bs = b * scale
        d = bs * gain[:, cols] - v * other
        dgain[:, cols] = jnp.sum(bs * v, axis=0, keepdims=True)
        g = gate[HALO:, cols]
        s = sigmoid(g)
        dm = d * (g * s)
        dy[:, cols] = dm
        dgate[:, cols] = (d * mixed[:, cols] * (s * (1.0 + g * (1.0 - s)))).astype(BF16)
        carried[cols, :] = fine(spread(inflow, j, size) * dm, read, 0, 0).astype(BF16)


def within_back_kernel(dims, act, xs, cum, hide, dy, dxs, dmaps):
    tokens, inner, state, lags, size = dims
    write, read = (act[:, inner : inner + state], act[:, inner + state :])
    scores = fine(read, write, 1, 1)
    sums = cum[...]
    sums_t = sums.T
    hidden = hide[...]
    lane = lax.broadcasted_iota(jnp.int32, (tokens, LANES), 1)
    per = LANES // size
    dscores = jnp.zeros((tokens, tokens), F32)
    for j, cols in tiles_of(inner):
        x = xs[:, cols]
        d = dy[:, cols]
        out = None
        for k in range(per):
            h = j * per + k
            decay = jnp.exp(sums[:, h : h + 1] - sums_t[h : h + 1, :] + hidden)
            y = fine(scores * decay, d, 0, 0)
            out = y if k == 0 else jnp.where(lane >= k * size, y, out)
            own = jnp.where((lane >= k * size) & (lane < (k + 1) * size), d, 0.0)
            dscores = dscores + fine(own, x, 1, 1) * decay
        dxs[:, cols] = out
    dmaps[:, :state] = fine(dscores, read, 0, 0)
    dmaps[:, state:] = fine(dscores, write, 1, 0)


def finish_kernel(
    dims,
    dxs_within,
    dmaps_within,
    dy,
    xs,
    act,
    z,
    mixed,
    cum,
    step,
    step_pre,
    where_,
    heads,
    adjoint,
    incoming,
    dz,
    dmaps,
    dstep,
    dheads,
):
    tokens, inner, state, lags, size = dims
    write = act[:, inner : inner + state]
    sums, steps = (cum[...], step[...])
    last = sums[tokens - 1 :, :]
    inflow = jnp.exp(sums) * where_[:, INFLOW : INFLOW + 1]
    ending = jnp.exp(last - sums) * where_[:, CLOSING : CLOSING + 1]
    passing = inflow[tokens - 1 :, :]
    dwrite = dmaps_within[:, :state]
    dread = dmaps_within[:, state:]
    dcum = jnp.zeros((tokens, LANES), F32)
    dstep_size = jnp.zeros((tokens, LANES), F32)
    dlast = jnp.zeros((1, LANES), F32)
    dpass = jnp.zeros((1, LANES), F32)
    dskip = jnp.zeros((1, LANES), F32)
    skip = heads[SKIP : SKIP + 1, :]
    for j, cols in tiles_of(inner):
        pick = head_columns(j, size)
        x, v, d = (xs[:, cols], act[:, cols], dy[:, cols])
        later = adjoint[cols, :]
        earlier = incoming[cols, :]
        end = spread(ending, j, size)
        skipped = spread(skip, j, size)
        ends = end * x
        reach = fine(write, later, 1, 1)
        dx = dxs_within[:, cols] + end * reach
        dwrite = dwrite + fine(ends, later, 1, 0)
        dread = dread + fine(spread(inflow, j, size) * d, earlier, 1, 0)
        dvalue = spread(steps, j, size) * dx + skipped * d
        zt = z[:, cols]
        s = sigmoid(zt)
        dz[:, cols] = dvalue * (s * (1.0 + zt * (1.0 - s)))
        dcum = dcum + fine(d * (mixed[:, cols] - skipped * v) - x * dx, pick, 1, 0)
        dstep_size = dstep_size + fine(dx * v, pick, 1, 0)
        dlast = dlast + fine(jnp.sum(ends * reach, axis=0, keepdims=True), pick, 1, 0)
        dskip = dskip + fine(jnp.sum(d * v, axis=0, keepdims=True), pick, 1, 0)
        across = fine(later * earlier, pick, 0, 0)
        dpass = dpass + jnp.sum(across, axis=0, keepdims=True)
    row = lax.broadcasted_iota(jnp.int32, (tokens, LANES), 0)
    dcum = dcum + jnp.where(row == tokens - 1, dlast + passing * dpass, 0.0)
    dlog = fine(lower_ones(tokens), dcum, 0, 0)
    rate = -jnp.exp(heads[DECAY : DECAY + 1, :])
    pre = step_pre[HALO:, :] + heads[BIAS : BIAS + 1, :]
    head = lax.broadcasted_iota(jnp.int32, (tokens, LANES), 1)
    dpre = jnp.where(head < inner // size, (dstep_size + dlog * rate) * sigmoid(pre), 0.0)
    dstep[...] = dpre
    dmaps[:, :state] = dwrite.astype(BF16)
    dmaps[:, state:] = dread.astype(BF16)
    dheads[...] = jnp.zeros(dheads.shape, F32)
    dheads[BIAS : BIAS + 1, :] = jnp.sum(dpre, axis=0, keepdims=True)
    dheads[DECAY : DECAY + 1, :] = jnp.sum(dlog * steps, axis=0, keepdims=True) * rate
    dheads[SKIP : SKIP + 1, :] = dskip


def conv_back_kernel(
    dims, dz, dz_maps, dz_after, dgate, dstep, proj, where_, taps, dpre, dtaps, padded
):
    tokens, inner, state, lags, size = dims
    padded[:tokens, :inner] = dz[...]
    padded[:tokens, inner:] = dz_maps[...]
    padded[tokens:, :] = dz_after[...]
    dpre[:, :inner] = dgate[...]
    dpre[:, 2 * inner + 2 * state :] = dstep[...].astype(BF16)
    dtaps[...] = jnp.zeros(dtaps.shape, F32)
    for _, cols in tiles_of(inner + 2 * state):
        shifted_cols = slice(inner + cols.start, inner + cols.stop)
        d = padded[:tokens, cols]
        total = taps[lags - 1 : lags, cols] * d
        for a in range(1, lags):
            piece = taps[lags - 1 - a : lags - a, cols] * padded[a : a + tokens, cols]
            total = total + piece * where_[:, AHEAD + a : AHEAD + a + 1]
        dpre[:, shifted_cols] = total.astype(BF16)
        for k in range(lags):
            begin = HALO - lags + 1 + k
            piece = d * proj[begin : begin + tokens, shifted_cols]
            if k < lags - 1:
                piece = piece * where_[:, k : k + 1]
            dtaps[k : k + 1, cols] = jnp.sum(piece, axis=0, keepdims=True)
        dtaps[lags : lags + 1, cols] = jnp.sum(d, axis=0, keepdims=True)


def call(kernel, dims, outs, *args, scratch=(), flops=0):
    shapes = [jax.ShapeDtypeStruct(shape, kind) for shape, kind in outs]
    moved = sum(a.size * a.dtype.itemsize for a in args)
    moved += sum(s.size * s.dtype.itemsize for s in shapes)
    return pl.pallas_call(
        functools.partial(kernel, dims),
        out_shape=shapes,
        in_specs=[pl.BlockSpec(memory_space=pltpu.VMEM)] * len(args),
        out_specs=[pl.BlockSpec(memory_space=pltpu.VMEM)] * len(shapes),
        scratch_shapes=scratch,
        compiler_params=pltpu.CompilerParams(vmem_limit_bytes=48 << 20),
        cost_estimate=pl.CostEstimate(flops=flops, bytes_accessed=moved, transcendentals=0),
        name=kernel.__name__,
    )(*args)


def rms_normed(residual, gain):
    scale = lax.rsqrt(jnp.mean(residual * residual, axis=1, keepdims=True) + EPSILON)
    return (residual * scale * gain[None, :]).astype(BF16)


def prefix_factors(decays, place):
    peers = decays.shape[0]
    which = jnp.arange(peers)
    low, mid = (which[:, None], which[None, :])
    inside = (mid > low) & (mid < place)
    before = jnp.prod(jnp.where(inside[:, :, None], decays[None], 1.0), axis=1)
    before = jnp.where((which < place)[:, None], before, 0.0)
    inside = (mid < low) & (mid > place)
    after = jnp.prod(jnp.where(inside[:, :, None], decays[None], 1.0), axis=1)
    after = jnp.where((which > place)[:, None], after, 0.0)
    return (before, after)


def combined(factors, states):
    peers, heads = factors.shape
    split = states.reshape(peers, heads, -1, states.shape[-1]).astype(F32)
    return jnp.sum(factors[:, :, None, None] * split, axis=0).reshape(states.shape[1:])


def layer_forward(residual, place, weights, params, table, hide):
    w_cat, w_out = weights
    gain, taps, heads, gate_gain, dims = params
    tokens, inner, state, lags, size = dims
    head_count = inner // size
    halo = shifted(residual[tokens - HALO :], "ctx", 1)
    extended = jnp.concatenate([halo, residual], axis=0)
    normed_all = rms_normed(extended, gain)
    proj = mm(normed_all, w_cat, 1, 0)
    wide = inner + 2 * state
    z, act, xs, step, cum, closing = call(
        front_kernel,
        dims,
        [
            ((tokens, wide), F32),
            ((tokens, wide), F32),
            ((tokens, inner), F32),
            ((tokens, LANES), F32),
            ((tokens, LANES), F32),
            ((inner, state), F32),
        ],
        proj,
        table,
        taps,
        heads,
    )
    passing = (jnp.exp(cum[tokens - 1]) * table[tokens - 1, INFLOW])[:head_count]
    high = passing.astype(BF16)
    low = (passing - high.astype(F32)).astype(BF16)
    marks = jnp.concatenate([high[:, None], low[:, None]], axis=1)
    marks = jnp.pad(marks, ((0, 0), (0, state - 2)))
    sent = jnp.concatenate([closing.astype(BF16), marks], axis=0)
    everyone = lax.all_gather(sent, "ctx")
    (within,) = call(
        within_kernel, dims, [((tokens, inner), F32)], act, xs, cum, hide, heads, flops=10**9
    )
    marks = everyone[:, inner:, :2].astype(F32)
    before, after = prefix_factors(marks[:, :, 0] + marks[:, :, 1], place)
    incoming = combined(before, everyone[:, :inner])
    mixed, gated, squares = call(
        join_kernel,
        dims,
        [((tokens, inner), F32), ((tokens, inner), F32), ((8, tokens), F32)],
        within,
        act,
        incoming,
        cum,
        table,
        proj,
    )
    width = inner * lax.axis_size("tp")
    scaling = lax.rsqrt(pair_sum(squares[0], "tp") / width + EPSILON)
    branch = (gated * scaling[:, None] * gate_gain[None, :]).astype(BF16)
    updated = residual + pair_sum(mm(branch, w_out, 1, 1), "tp")
    saved = (
        normed_all[HALO:],
        branch,
        gated,
        mixed,
        scaling,
        proj,
        z,
        act,
        xs,
        step,
        cum,
        incoming,
        after,
    )
    return (updated, saved)


def layer_backward(upstream, residual, saved, weights, params, table, hide, mine):
    w_cat, w_out = weights
    gain, taps, heads, gate_gain, dims = params
    tokens, inner, state, lags, size = dims
    normed, branch, gated, mixed, scaling, proj, z, act, xs, step, cum, incoming, after = saved
    width = inner * lax.axis_size("tp")
    wide = inner + 2 * state
    outward = upstream.astype(BF16)
    pulled = mm(outward, w_out, 1, 0)
    inward = pair_sum(jnp.sum(pulled * gate_gain[None, :] * gated, axis=1), "tp")
    grad_out = mm(outward, branch, 0, 0).astype(BF16)
    factors = jnp.stack([scaling, scaling * scaling * scaling * inward / width], axis=1)
    factors = jnp.pad(factors, ((0, 0), (0, LANES - 2)))
    dy, dgate, carried, dgain = call(
        gate_back_kernel,
        dims,
        [
            ((tokens, inner), F32),
            ((tokens, inner), BF16),
            ((inner, state), BF16),
            ((1, inner), F32),
        ],
        pulled,
        gated,
        mixed,
        proj,
        factors,
        gate_gain[None, :],
        act,
        cum,
        table,
    )
    everyone = lax.all_gather(carried, "ctx")
    dxs, dmaps = call(
        within_back_kernel,
        dims,
        [((tokens, inner), F32), ((tokens, 2 * state), F32)],
        act,
        xs,
        cum,
        hide,
        dy,
        flops=2 * 10**9,
    )
    adjoint = combined(after, everyone)
    dz, dmaps, dstep, dheads = call(
        finish_kernel,
        dims,
        [
            ((tokens, inner), F32),
            ((tokens, 2 * state), BF16),
            ((tokens, LANES), F32),
            ((8, LANES), F32),
        ],
        dxs,
        dmaps,
        dy,
        xs,
        act,
        z,
        mixed,
        cum,
        step,
        proj[:, 2 * inner + 2 * state :],
        table,
        heads,
        adjoint,
        incoming,
    )
    z_maps = z[:, inner:]
    s = sigmoid(z_maps)
    dz_maps = pair_sum(dmaps, "tp") * (s * (1.0 + z_maps * (1.0 - s)))
    first = jnp.concatenate([dz[:HALO], dz_maps[:HALO]], axis=1)
    dz_after = shifted(first, "ctx", -1)
    dpre, dtaps = call(
        conv_back_kernel,
        dims,
        [((tokens, w_cat.shape[1]), BF16), ((8, wide), F32)],
        dz,
        dz_maps,
        dz_after,
        dgate,
        dstep,
        proj,
        table,
        taps,
        scratch=[pltpu.VMEM((tokens + HALO, wide), F32)],
    )
    partial = mm(dpre * mine[None, :], w_cat, 1, 1).astype(BF16)
    grad_normed = pair_sum(partial, "tp")
    grad_cat = mm(normed, dpre, 0, 0).astype(BF16)
    shards = (
        lax.psum_scatter(grad_cat, ROWS, scatter_dimension=0, tiled=True),
        lax.psum_scatter(grad_out, ROWS, scatter_dimension=0, tiled=True),
    )
    scale = lax.rsqrt(jnp.mean(residual * residual, axis=1, keepdims=True) + EPSILON)
    grad_gain = jnp.sum(grad_normed * residual * scale, axis=0)
    pull = grad_normed * gain[None, :]
    along = jnp.mean(pull * residual, axis=1, keepdims=True)
    upstream = upstream + pull * scale - residual * (scale * scale * scale * along)
    small = jnp.concatenate(
        [
            grad_gain.reshape(-1, LANES),
            dtaps[: lags + 1].reshape(-1, LANES),
            dheads[:3],
            dgain.reshape(-1, LANES),
        ],
        axis=0,
    )
    return (upstream, shards, small)


def on_device(
    hidden_in,
    segments,
    cotangent,
    norm_gain,
    in_proj,
    step_proj,
    state_proj,
    out_proj,
    conv_inner,
    inner_bias,
    conv_state,
    state_bias,
    step_bias,
    decay_log,
    skip_scale,
    gate_gain,
):
    layer_count, rows, _, inner = in_proj.shape
    tokens = segments.shape[1]
    model = hidden_in.shape[2]
    lags = conv_inner.shape[1]
    state = state_proj.shape[2] // 2
    head_count = step_proj.shape[2]
    size = inner // head_count
    wide = inner + 2 * state
    dims = (tokens, inner, state, lags, size)
    place = lax.axis_index("ctx")

    gathered = []
    for l in range(layer_count):
        steps = jnp.pad(step_proj[l], ((0, 0), (0, LANES - head_count)))
        packed = jnp.concatenate(
            [in_proj[l].reshape(rows, 2 * inner), state_proj[l], steps], axis=1
        )
        w_cat = lax.all_gather(packed, ROWS, axis=0, tiled=True)
        w_out = lax.all_gather(out_proj[l], ROWS, axis=0, tiled=True)
        gathered.append((w_cat, w_out))

    per_shard = norm_gain.shape[0]
    heads_in = jnp.stack([step_bias, decay_log, skip_scale], axis=1)
    heads_in = jnp.pad(heads_in, ((0, 0), (0, 5), (0, LANES - head_count)))
    taps_in = jnp.concatenate(
        [
            jnp.concatenate([conv_inner, conv_state], axis=2),
            jnp.concatenate([inner_bias, state_bias], axis=1)[:, None, :],
        ],
        axis=1,
    )
    flat = jnp.concatenate(
        [
            norm_gain.reshape(per_shard, -1, LANES),
            gate_gain.reshape(per_shard, -1, LANES),
            taps_in.reshape(per_shard, -1, LANES),
            heads_in,
        ],
        axis=1,
    )
    flat = lax.all_gather(flat, "fsdp", axis=0, tiled=True)
    a = model // LANES
    b = a + inner // LANES
    c = b + (lags + 1) * wide // LANES

    labels = segments[0]
    fore = shifted(labels[tokens - HALO :], "ctx", 1)
    aft = shifted(labels[:HALO], "ctx", -1)
    around = jnp.concatenate([fore, labels, aft], axis=0)
    columns = [jnp.zeros((tokens,), F32)] * LANES
    for k in range(lags - 1):
        begin = HALO - lags + 1 + k
        columns[k] = (around[begin : begin + tokens] == labels).astype(F32)
    for k in range(1, lags):
        columns[AHEAD + k] = (around[HALO + k : HALO + k + tokens] == labels).astype(F32)
    columns[INFLOW] = (labels == fore[HALO - 1]).astype(F32)
    columns[CLOSING] = (labels == labels[tokens - 1]).astype(F32)
    table = jnp.stack(columns, axis=1)
    at = jnp.arange(tokens)
    visible = (at[:, None] >= at[None, :]) & (labels[:, None] == labels[None, :])
    hide = jnp.where(visible, 0.0, HIDE).astype(F32)

    pairs = lax.axis_size("tp")
    column = jnp.arange(2 * inner + 2 * state + LANES)
    shared = (column >= 2 * inner) & (column < 2 * inner + 2 * state)
    owner = (column - 2 * inner) * pairs // (2 * state)
    mine = (~shared | (owner == lax.axis_index("tp"))).astype(BF16)

    residual = hidden_in[0].astype(F32)
    residuals, records, layer_params = ([], [], [])
    for l in range(layer_count):
        taps = jnp.pad(flat[l, b:c].reshape(lags + 1, wide), ((0, 7 - lags), (0, 0)))
        params = (flat[l, :a].reshape(-1), taps, flat[l, c:], flat[l, a:b].reshape(-1), dims)
        residuals.append(residual)
        residual, saved = layer_forward(residual, place, gathered[l], params, table, hide)
        records.append(saved)
        layer_params.append(params)
    hidden_out = residual.astype(BF16)[None]

    upstream = cotangent[0].astype(F32)
    cats, outs, smalls = ([None] * layer_count for _ in range(3))
    for l in reversed(range(layer_count)):
        upstream, shards, smalls[l] = layer_backward(
            upstream, residuals[l], records[l], gathered[l], layer_params[l], table, hide, mine
        )
        cats[l], outs[l] = shards

    cat = jnp.stack(cats, axis=0).astype(F32)
    grad_in = cat[:, :, : 2 * inner].reshape(in_proj.shape)
    grad_state = cat[:, :, 2 * inner : 2 * inner + 2 * state]
    grad_step = cat[:, :, 2 * inner + 2 * state : 2 * inner + 2 * state + head_count]
    grad_out = jnp.stack(outs, axis=0).astype(F32)

    small = jnp.stack(smalls, axis=0)
    pieces = lax.all_gather(small, ROWS)
    first_layer = lax.axis_index("fsdp") * per_shard
    small = jnp.sum(lax.dynamic_slice_in_dim(pieces, first_layer, per_shard, 1), axis=0)
    d = a + (lags + 1) * wide // LANES
    taps_out = small[:, a:d].reshape(per_shard, lags + 1, wide)
    heads_out = small[:, d : d + 3, :head_count]
    return (
        hidden_out,
        upstream[None],
        small[:, :a].reshape(per_shard, model),
        grad_in,
        grad_step,
        grad_state,
        grad_out,
        taps_out[:, :lags, :inner],
        taps_out[:, lags, :inner],
        taps_out[:, :lags, inner:],
        taps_out[:, lags, inner:],
        heads_out[:, BIAS],
        heads_out[:, DECAY],
        heads_out[:, SKIP],
        small[:, d + 3 :].reshape(per_shard, inner),
    )


def solution(mesh):
    wide, thin = (P("fsdp", "ctx", None), P("fsdp", "tp"))
    weights = (
        P(None, ROWS, None, "tp"),
        P(None, ROWS, "tp"),
        P(None, ROWS, None),
        P(None, ROWS, "tp"),
    )
    small = (
        P("fsdp", None, "tp"),
        thin,
        P("fsdp", None, None),
        P("fsdp", None),
        thin,
        thin,
        thin,
        thin,
    )
    return jax.shard_map(
        on_device,
        mesh=mesh,
        in_specs=(wide, P("fsdp", "ctx"), wide, P("fsdp", None)) + weights + small,
        out_specs=(wide, wide, P("fsdp", None)) + weights + small,
        check_vma=False,
    )
```

```python
import functools

import jax
import jax.numpy as jnp
from jax import lax
from jax.experimental import pallas as pl
from jax.experimental.pallas import tpu as pltpu
from jax.sharding import PartitionSpec as P

EPSILON = 1e-05
HIGHEST = lax.Precision.HIGHEST
LANES = 128
HALO = 8
ROWS = ("fsdp", "ctx")
HIDE = -1e30
F32 = jnp.float32
BF16 = jnp.bfloat16

INFLOW, CLOSING, AHEAD = 8, 9, 16
BIAS, DECAY, SKIP = 0, 1, 2


def shifted(block, axis, distance):
    devices = range(lax.axis_size(axis))
    route = [(i - distance, i) for i in devices if i - distance in devices]
    return lax.ppermute(block, axis, route)


def swapped(block, axis):
    count = lax.axis_size(axis)
    return lax.ppermute(block, axis, [(i, (i + 1) % count) for i in range(count)])


def pair_sum(block, axis):
    total, moving = (block.astype(F32), block)
    for _ in range(lax.axis_size(axis) - 1):
        moving = swapped(moving, axis)
        total = total + moving.astype(F32)
    return total


def bits(axis):
    count = lax.axis_size(axis)
    assert count & (count - 1) == 0
    return [(axis, 1 << k) for k in range(count.bit_length() - 1)]


def partner(block, axis, bit):
    return lax.ppermute(block, axis, [(i, i ^ bit) for i in range(lax.axis_size(axis))])


def side(axis, bit):
    return (lax.axis_index(axis) // bit) % 2


def shard_bits():
    return bits("fsdp")[::-1] + bits("ctx")[::-1]


def halved_scatter(block, order):
    left = shard_bits()
    block = block.reshape((2,) * len(left) + (-1, block.shape[1]))
    for axis, bit in order:
        dim = left.index((axis, bit))
        mine = side(axis, bit)
        away = lax.dynamic_index_in_dim(block, 1 - mine, dim, False)
        kept = lax.dynamic_index_in_dim(block, mine, dim, False)
        left.remove((axis, bit))
        block = kept.astype(F32) + partner(away, axis, bit).astype(F32)
        block = block.astype(BF16) if left else block
    return block


def doubled_gather(block, order):
    every = shard_bits()
    have = []
    for axis, bit in order:
        other = partner(block, axis, bit)
        have = [b for b in every if b in have or b == (axis, bit)]
        dim = have.index((axis, bit))
        low = side(axis, bit) == 0
        first = jnp.where(low, block, other)
        second = jnp.where(low, other, block)
        block = jnp.stack([first, second], axis=dim)
    return block.reshape(-1, block.shape[-1])


def exchanged_sum(block):
    for axis, bit in shard_bits():
        block = block + partner(block, axis, bit)
    return block


def scattered(block):
    (ys, cs) = (bits("fsdp"), bits("ctx"))
    first = ys + cs
    second = cs[:1] + ys + cs[1:]
    cut = block.shape[1] // (2 * LANES) * LANES
    return jnp.concatenate(
        [halved_scatter(block[:, :cut], first), halved_scatter(block[:, cut:], second)], axis=1
    )


def mm(a, b, ca, cb):
    return lax.dot_general(a, b, (((ca,), (cb,)), ((), ())), preferred_element_type=F32)


def fine(a, b, ca, cb):
    return lax.dot_general(
        a, b, (((ca,), (cb,)), ((), ())), precision=HIGHEST, preferred_element_type=F32
    )


def sigmoid(v):
    return 1.0 / (1.0 + jnp.exp(-v))


def lower_ones(length):
    row = lax.broadcasted_iota(jnp.int32, (length, length), 0)
    col = lax.broadcasted_iota(jnp.int32, (length, length), 1)
    return (row >= col).astype(F32)


def spread(table, tile, size):
    per = LANES // size
    lane = lax.broadcasted_iota(jnp.int32, (table.shape[0], LANES), 1)
    first = tile * per
    out = jnp.broadcast_to(table[:, first : first + 1], lane.shape)
    for k in range(1, per):
        column = jnp.broadcast_to(table[:, first + k : first + k + 1], lane.shape)
        out = jnp.where(lane >= k * size, column, out)
    return out


def head_columns(tile, size):
    row = lax.broadcasted_iota(jnp.int32, (LANES, LANES), 0)
    col = lax.broadcasted_iota(jnp.int32, (LANES, LANES), 1)
    return (row // size + tile * (LANES // size) == col).astype(F32)


def tiles_of(width):
    return [(j, slice(j * LANES, (j + 1) * LANES)) for j in range(width // LANES)]


def step_sizes(pre, bias):
    v = pre + bias
    return jnp.maximum(v, 0.0) + jnp.log1p(jnp.exp(-jnp.abs(v)))


def put_decay(packed, inner, decay):
    high = decay.astype(BF16).astype(F32)
    row = lax.broadcasted_iota(jnp.int32, (16, LANES), 0)
    packed[inner:, :] = jnp.where(row < 8, high, decay - high).astype(BF16)


def get_decay(packed, inner):
    both = packed[inner:, :].astype(F32)
    return both[0:1, :] + both[8:9, :]


def head_rows(decay, tile, size):
    return jnp.sum(head_columns(tile, size) * decay, axis=1, keepdims=True)


def chained(parts, inner, size, j, cols):
    total, factor = (parts[0][cols, :].astype(F32), get_decay(parts[0], inner))
    for part in parts[1:]:
        total = total + head_rows(factor, j, size) * part[cols, :].astype(F32)
        factor = factor * get_decay(part, inner)
    return (total, factor)


def fold_kernel(dims, *refs):
    inner, size = (dims[1], dims[4])
    parts, packed = (refs[:-1], refs[-1])
    factor = None
    for j, cols in tiles_of(inner):
        total, factor = chained(parts, inner, size, j, cols)
        packed[cols, :] = total.astype(BF16)
    put_decay(packed, inner, factor)


def front_kernel(dims, proj, where_, taps, heads, z, act, xs, step, cum, closing):
    tokens, inner, state, lags, size = dims
    for _, cols in tiles_of(inner + 2 * state):
        source = slice(inner + cols.start, inner + cols.stop)
        total = jnp.broadcast_to(taps[lags : lags + 1, cols], (tokens, LANES))
        for k in range(lags):
            begin = HALO - lags + 1 + k
            piece = taps[k : k + 1, cols] * proj[begin : begin + tokens, source]
            if k < lags - 1:
                piece = piece * where_[:, k : k + 1]
            total = total + piece
        z[:, cols] = total
        act[:, cols] = total * sigmoid(total)
    steps = step_sizes(proj[HALO:, 2 * inner + 2 * state :], heads[BIAS : BIAS + 1, :])
    rate = -jnp.exp(heads[DECAY : DECAY + 1, :])
    summed = fine(lower_ones(tokens), steps * rate, 1, 0)
    step[...] = steps
    cum[...] = summed
    ending = jnp.exp(summed[tokens - 1 :, :] - summed) * where_[:, CLOSING : CLOSING + 1]
    write = act[:, inner : inner + state]
    for j, cols in tiles_of(inner):
        scaled = act[:, cols] * spread(steps, j, size)
        xs[:, cols] = scaled
        closing[cols, :] = fine(scaled * spread(ending, j, size), write, 0, 0).astype(BF16)
    entering = where_[tokens - 1 :, INFLOW : INFLOW + 1]
    put_decay(closing, inner, jnp.exp(summed[tokens - 1 :, :]) * entering)


def within_kernel(dims, act, xs, cum, hide, heads, within):
    tokens, inner, state, lags, size = dims
    write, read = (act[:, inner : inner + state], act[:, inner + state :])
    scores = fine(read, write, 1, 1)
    sums = cum[...]
    sums_t = sums.T
    hidden = hide[...]
    lane = lax.broadcasted_iota(jnp.int32, (tokens, LANES), 1)
    per = LANES // size
    for j, cols in tiles_of(inner):
        x = xs[:, cols]
        out = None
        for k in range(per):
            h = j * per + k
            decay = jnp.exp(sums[:, h : h + 1] - sums_t[h : h + 1, :] + hidden)
            y = fine(scores * decay, x, 1, 0)
            out = y if k == 0 else jnp.where(lane >= k * size, y, out)
        within[:, cols] = out + spread(heads[SKIP : SKIP + 1, :], j, size) * act[:, cols]


def join_kernel(dims, within, act, cum, where_, gate, *refs):
    tokens, inner, state, lags, size = dims
    parts, (mixed, gated, squares, incoming) = (refs[:-4], refs[-4:])
    read = act[:, inner + state :]
    inflow = jnp.exp(cum[...]) * where_[:, INFLOW : INFLOW + 1]
    total = jnp.zeros((tokens, LANES), F32)
    for j, cols in tiles_of(inner):
        entered, _ = chained(parts, inner, size, j, cols)
        incoming[cols, :] = entered
        reached = fine(read, entered, 1, 1)
        m = within[:, cols] + spread(inflow, j, size) * reached
        g = gate[HALO:, cols]
        v = m * (g * sigmoid(g))
        mixed[:, cols] = m
        gated[:, cols] = v
        total = total + v * v
    squares[...] = fine(jnp.ones((8, LANES), F32), total, 1, 1)


def gate_back_kernel(
    dims, pulled, gated, mixed, gate, factors, gain, act, cum, where_, dy, dgate, carried, dgain
):
    tokens, inner, state, lags, size = dims
    scale, other = (factors[:, 0:1], factors[:, 1:2])
    read = act[:, inner + state :]
    inflow = jnp.exp(cum[...]) * where_[:, INFLOW : INFLOW + 1]
    for j, cols in tiles_of(inner):
        b = pulled[:, cols]
        v = gated[:, cols]
        bs = b * scale
        d = bs * gain[:, cols] - v * other
        dgain[:, cols] = jnp.sum(bs * v, axis=0, keepdims=True)
        g = gate[HALO:, cols]
        s = sigmoid(g)
        dm = d * (g * s)
        dy[:, cols] = dm
        dgate[:, cols] = (d * mixed[:, cols] * (s * (1.0 + g * (1.0 - s)))).astype(BF16)
        carried[cols, :] = fine(spread(inflow, j, size) * dm, read, 0, 0).astype(BF16)
    put_decay(carried, inner, inflow[tokens - 1 :, :])


def within_back_kernel(dims, act, xs, cum, hide, dy, dxs, dmaps):
    tokens, inner, state, lags, size = dims
    write, read = (act[:, inner : inner + state], act[:, inner + state :])
    scores = fine(read, write, 1, 1)
    sums = cum[...]
    sums_t = sums.T
    hidden = hide[...]
    lane = lax.broadcasted_iota(jnp.int32, (tokens, LANES), 1)
    per = LANES // size
    dscores = jnp.zeros((tokens, tokens), F32)
    for j, cols in tiles_of(inner):
        x = xs[:, cols]
        d = dy[:, cols]
        out = None
        for k in range(per):
            h = j * per + k
            decay = jnp.exp(sums[:, h : h + 1] - sums_t[h : h + 1, :] + hidden)
            y = fine(scores * decay, d, 0, 0)
            out = y if k == 0 else jnp.where(lane >= k * size, y, out)
            own = jnp.where((lane >= k * size) & (lane < (k + 1) * size), d, 0.0)
            dscores = dscores + fine(own, x, 1, 1) * decay
        dxs[:, cols] = out
    dmaps[:, :state] = fine(dscores, read, 0, 0)
    dmaps[:, state:] = fine(dscores, write, 1, 0)


def finish_kernel(
    dims,
    dxs_within,
    dmaps_within,
    dy,
    xs,
    act,
    z,
    mixed,
    cum,
    step,
    step_pre,
    where_,
    heads,
    incoming,
    *refs,
):
    tokens, inner, state, lags, size = dims
    parts, (dz, dmaps, dstep, dheads) = (refs[:-4], refs[-4:])
    write = act[:, inner : inner + state]
    sums, steps = (cum[...], step[...])
    last = sums[tokens - 1 :, :]
    inflow = jnp.exp(sums) * where_[:, INFLOW : INFLOW + 1]
    ending = jnp.exp(last - sums) * where_[:, CLOSING : CLOSING + 1]
    passing = inflow[tokens - 1 :, :]
    dwrite = dmaps_within[:, :state]
    dread = dmaps_within[:, state:]
    dcum = jnp.zeros((tokens, LANES), F32)
    dstep_size = jnp.zeros((tokens, LANES), F32)
    dlast = jnp.zeros((1, LANES), F32)
    dpass = jnp.zeros((1, LANES), F32)
    dskip = jnp.zeros((1, LANES), F32)
    skip = heads[SKIP : SKIP + 1, :]
    for j, cols in tiles_of(inner):
        pick = head_columns(j, size)
        x, v, d = (xs[:, cols], act[:, cols], dy[:, cols])
        later, _ = chained(parts, inner, size, j, cols)
        earlier = incoming[cols, :]
        end = spread(ending, j, size)
        skipped = spread(skip, j, size)
        ends = end * x
        reach = fine(write, later, 1, 1)
        dx = dxs_within[:, cols] + end * reach
        dwrite = dwrite + fine(ends, later, 1, 0)
        dread = dread + fine(spread(inflow, j, size) * d, earlier, 1, 0)
        dvalue = spread(steps, j, size) * dx + skipped * d
        zt = z[:, cols]
        s = sigmoid(zt)
        dz[:, cols] = dvalue * (s * (1.0 + zt * (1.0 - s)))
        dcum = dcum + fine(d * (mixed[:, cols] - skipped * v) - x * dx, pick, 1, 0)
        dstep_size = dstep_size + fine(dx * v, pick, 1, 0)
        dlast = dlast + fine(jnp.sum(ends * reach, axis=0, keepdims=True), pick, 1, 0)
        dskip = dskip + fine(jnp.sum(d * v, axis=0, keepdims=True), pick, 1, 0)
        across = fine(later * earlier, pick, 0, 0)
        dpass = dpass + jnp.sum(across, axis=0, keepdims=True)
    row = lax.broadcasted_iota(jnp.int32, (tokens, LANES), 0)
    dcum = dcum + jnp.where(row == tokens - 1, dlast + passing * dpass, 0.0)
    dlog = fine(lower_ones(tokens), dcum, 0, 0)
    rate = -jnp.exp(heads[DECAY : DECAY + 1, :])
    pre = step_pre[HALO:, :] + heads[BIAS : BIAS + 1, :]
    head = lax.broadcasted_iota(jnp.int32, (tokens, LANES), 1)
    dpre = jnp.where(head < inner // size, (dstep_size + dlog * rate) * sigmoid(pre), 0.0)
    dstep[...] = dpre
    dmaps[:, :state] = dwrite.astype(BF16)
    dmaps[:, state:] = dread.astype(BF16)
    dheads[...] = jnp.zeros(dheads.shape, F32)
    dheads[BIAS : BIAS + 1, :] = jnp.sum(dpre, axis=0, keepdims=True)
    dheads[DECAY : DECAY + 1, :] = jnp.sum(dlog * steps, axis=0, keepdims=True) * rate
    dheads[SKIP : SKIP + 1, :] = dskip


def conv_back_kernel(
    dims, dz, dz_maps, dz_after, dstep, proj, where_, taps, dpre, dtaps, padded
):
    tokens, inner, state, lags, size = dims
    padded[:tokens, :inner] = dz[...]
    padded[:tokens, inner:] = dz_maps[...]
    padded[tokens:, :] = dz_after[...]
    dpre[:, inner + 2 * state :] = dstep[...].astype(BF16)
    dtaps[...] = jnp.zeros(dtaps.shape, F32)
    for _, cols in tiles_of(inner + 2 * state):
        shifted_cols = slice(inner + cols.start, inner + cols.stop)
        d = padded[:tokens, cols]
        total = taps[lags - 1 : lags, cols] * d
        for a in range(1, lags):
            piece = taps[lags - 1 - a : lags - a, cols] * padded[a : a + tokens, cols]
            total = total + piece * where_[:, AHEAD + a : AHEAD + a + 1]
        dpre[:, cols] = total.astype(BF16)
        for k in range(lags):
            begin = HALO - lags + 1 + k
            piece = d * proj[begin : begin + tokens, shifted_cols]
            if k < lags - 1:
                piece = piece * where_[:, k : k + 1]
            dtaps[k : k + 1, cols] = jnp.sum(piece, axis=0, keepdims=True)
        dtaps[lags : lags + 1, cols] = jnp.sum(d, axis=0, keepdims=True)


def call(kernel, dims, outs, *args, scratch=(), flops=0):
    shapes = [jax.ShapeDtypeStruct(shape, kind) for shape, kind in outs]
    moved = sum(a.size * a.dtype.itemsize for a in args)
    moved += sum(s.size * s.dtype.itemsize for s in shapes)
    return pl.pallas_call(
        functools.partial(kernel, dims),
        out_shape=shapes,
        in_specs=[pl.BlockSpec(memory_space=pltpu.VMEM)] * len(args),
        out_specs=[pl.BlockSpec(memory_space=pltpu.VMEM)] * len(shapes),
        scratch_shapes=scratch,
        compiler_params=pltpu.CompilerParams(vmem_limit_bytes=48 << 20),
        cost_estimate=pl.CostEstimate(flops=flops, bytes_accessed=moved, transcendentals=0),
        name=kernel.__name__,
    )(*args)


def rms_normed(residual, gain):
    scale = lax.rsqrt(jnp.mean(residual * residual, axis=1, keepdims=True) + EPSILON)
    return (residual * scale * gain[None, :]).astype(BF16)


def carried_over(packed, direction, dims):
    reach = max(lax.axis_size("ctx") // 2, 1)
    far = shifted(packed, "ctx", direction * reach)
    parts, sending = ([], packed)
    while len(parts) < reach.bit_length() - 1:
        parts.append(shifted(sending, "ctx", direction << len(parts)))
        if len(parts) < reach.bit_length() - 1:
            (sending,) = call(fold_kernel, dims, [(packed.shape, BF16)], packed, *parts)
    return parts + [far]


def layer_forward(residual, weights, params, table, hide):
    w_cat, w_out = weights
    gain, taps, heads, gate_gain, dims = params
    tokens, inner, state, lags, size = dims
    head_count = inner // size
    halo = shifted(residual[tokens - HALO :], "ctx", 1)
    extended = jnp.concatenate([halo, residual], axis=0)
    normed_all = rms_normed(extended, gain)
    proj = mm(normed_all, w_cat, 1, 0)
    wide = inner + 2 * state
    z, act, xs, step, cum, closing = call(
        front_kernel,
        dims,
        [
            ((tokens, wide), F32),
            ((tokens, wide), F32),
            ((tokens, inner), F32),
            ((tokens, LANES), F32),
            ((tokens, LANES), F32),
            ((inner + 16, state), BF16),
        ],
        proj,
        table,
        taps,
        heads,
    )
    parts = carried_over(closing, 1, dims)
    (within,) = call(
        within_kernel, dims, [((tokens, inner), F32)], act, xs, cum, hide, heads, flops=10**9
    )
    mixed, gated, squares, incoming = call(
        join_kernel,
        dims,
        [
            ((tokens, inner), F32),
            ((tokens, inner), F32),
            ((8, tokens), F32),
            ((inner, state), F32),
        ],
        within,
        act,
        cum,
        table,
        proj,
        *parts,
    )
    width = inner * lax.axis_size("tp")
    scaling = lax.rsqrt(pair_sum(squares[0], "tp") / width + EPSILON)
    branch = (gated * scaling[:, None] * gate_gain[None, :]).astype(BF16)
    updated = residual + pair_sum(mm(branch, w_out, 1, 1), "tp")
    saved = (
        normed_all[HALO:],
        branch,
        gated,
        mixed,
        scaling,
        proj,
        z,
        act,
        xs,
        step,
        cum,
        incoming,
    )
    return (updated, saved)


def layer_backward(upstream, residual, saved, weights, params, table, hide, mine, last):
    w_cat, w_out = weights
    gain, taps, heads, gate_gain, dims = params
    tokens, inner, state, lags, size = dims
    normed, branch, gated, mixed, scaling, proj, z, act, xs, step, cum, incoming = saved
    width = inner * lax.axis_size("tp")
    wide = inner + 2 * state
    outward = upstream.astype(BF16)
    pulled = mm(outward, w_out, 1, 0)
    inward = pair_sum(jnp.sum(pulled * gate_gain[None, :] * gated, axis=1), "tp")
    grad_out = mm(outward, branch, 0, 0).astype(BF16)
    factors = jnp.stack([scaling, scaling * scaling * scaling * inward / width], axis=1)
    factors = jnp.pad(factors, ((0, 0), (0, LANES - 2)))
    dy, dgate, carried, dgain = call(
        gate_back_kernel,
        dims,
        [
            ((tokens, inner), F32),
            ((tokens, inner), BF16),
            ((inner + 16, state), BF16),
            ((1, inner), F32),
        ],
        pulled,
        gated,
        mixed,
        proj,
        factors,
        gate_gain[None, :],
        act,
        cum,
        table,
    )
    parts = carried_over(carried, -1, dims)
    dxs, dmaps = call(
        within_back_kernel,
        dims,
        [((tokens, inner), F32), ((tokens, 2 * state), F32)],
        act,
        xs,
        cum,
        hide,
        dy,
        flops=2 * 10**9,
    )
    dz, dmaps, dstep, dheads = call(
        finish_kernel,
        dims,
        [
            ((tokens, inner), F32),
            ((tokens, 2 * state), BF16),
            ((tokens, LANES), F32),
            ((8, LANES), F32),
        ],
        dxs,
        dmaps,
        dy,
        xs,
        act,
        z,
        mixed,
        cum,
        step,
        proj[:, 2 * inner + 2 * state :],
        table,
        heads,
        incoming,
        *parts,
    )
    z_maps = z[:, inner:]
    s = sigmoid(z_maps)
    dz_maps = pair_sum(dmaps, "tp") * (s * (1.0 + z_maps * (1.0 - s)))
    first = jnp.concatenate([dz[:HALO], dz_maps[:HALO]], axis=1)
    dz_after = shifted(first, "ctx", -1)
    dpre, dtaps = call(
        conv_back_kernel,
        dims,
        [((tokens, wide + LANES), BF16), ((8, wide), F32)],
        dz,
        dz_maps,
        dz_after,
        dstep,
        proj,
        table,
        taps,
        scratch=[pltpu.VMEM((tokens + HALO, wide), F32)],
    )
    partial = mm(dgate, w_cat[:, :inner], 1, 1) + mm(dpre * mine[None, :], w_cat[:, inner:], 1, 1)
    grad_normed = pair_sum(partial.astype(BF16), "tp")
    grad_gate = mm(normed, dgate, 0, 0).astype(BF16)
    grad_rest = mm(normed, dpre, 0, 0).astype(BF16)
    if last:
        whole = jnp.concatenate([grad_gate, grad_rest, grad_out], axis=1)
        shard = lax.psum_scatter(whole, ROWS, scatter_dimension=0, tiled=True).astype(F32)
    else:
        early = scattered(jnp.concatenate([grad_out, grad_gate], axis=1))
        shard = jnp.concatenate(
            [early[:, inner:], scattered(grad_rest), early[:, :inner]], axis=1
        )
    scale = lax.rsqrt(jnp.mean(residual * residual, axis=1, keepdims=True) + EPSILON)
    grad_gain = jnp.sum(grad_normed * residual * scale, axis=0)
    pull = grad_normed * gain[None, :]
    along = jnp.mean(pull * residual, axis=1, keepdims=True)
    upstream = upstream + pull * scale - residual * (scale * scale * scale * along)
    small = jnp.concatenate(
        [
            grad_gain.reshape(-1, LANES),
            dtaps[: lags + 1].reshape(-1, LANES),
            dheads[:3],
            dgain.reshape(-1, LANES),
        ],
        axis=0,
    )
    return (upstream, shard, small)


def on_device(
    hidden_in,
    segments,
    cotangent,
    norm_gain,
    in_proj,
    step_proj,
    state_proj,
    out_proj,
    conv_inner,
    inner_bias,
    conv_state,
    state_bias,
    step_bias,
    decay_log,
    skip_scale,
    gate_gain,
):
    layer_count, rows, _, inner = in_proj.shape
    tokens = segments.shape[1]
    model = hidden_in.shape[2]
    lags = conv_inner.shape[1]
    state = state_proj.shape[2] // 2
    head_count = step_proj.shape[2]
    size = inner // head_count
    wide = inner + 2 * state
    dims = (tokens, inner, state, lags, size)

    gathered = []
    for l in range(layer_count):
        steps = jnp.pad(step_proj[l], ((0, 0), (0, LANES - head_count)))
        packed = jnp.concatenate(
            [in_proj[l].reshape(rows, 2 * inner), state_proj[l], steps], axis=1
        )
        if l:
            packed = jnp.concatenate([packed, out_proj[l]], axis=1)
            packed = lax.all_gather(packed, ROWS, axis=0, tiled=True)
            w_cat, w_out = (packed[:, : packed.shape[1] - inner], packed[:, -inner:])
        else:
            w_cat = lax.all_gather(packed, ROWS, axis=0, tiled=True)
            w_out = doubled_gather(out_proj[l], bits("ctx")[::-1] + bits("fsdp"))
        gathered.append((w_cat, w_out))

    per_shard = norm_gain.shape[0]
    heads_in = jnp.stack([step_bias, decay_log, skip_scale], axis=1)
    heads_in = jnp.pad(heads_in, ((0, 0), (0, 5), (0, LANES - head_count)))
    taps_in = jnp.concatenate(
        [
            jnp.concatenate([conv_inner, conv_state], axis=2),
            jnp.concatenate([inner_bias, state_bias], axis=1)[:, None, :],
        ],
        axis=1,
    )
    flat = jnp.concatenate(
        [
            norm_gain.reshape(per_shard, -1, LANES),
            gate_gain.reshape(per_shard, -1, LANES),
            taps_in.reshape(per_shard, -1, LANES),
            heads_in,
        ],
        axis=1,
    )
    flat = lax.all_gather(flat, "fsdp", axis=0, tiled=True)
    a = model // LANES
    b = a + inner // LANES
    c = b + (lags + 1) * wide // LANES

    labels = segments[0]
    fore = shifted(labels[tokens - HALO :], "ctx", 1)
    aft = shifted(labels[:HALO], "ctx", -1)
    around = jnp.concatenate([fore, labels, aft], axis=0)
    columns = [jnp.zeros((tokens,), F32)] * LANES
    for k in range(lags - 1):
        begin = HALO - lags + 1 + k
        columns[k] = (around[begin : begin + tokens] == labels).astype(F32)
    for k in range(1, lags):
        columns[AHEAD + k] = (around[HALO + k : HALO + k + tokens] == labels).astype(F32)
    columns[INFLOW] = (labels == fore[HALO - 1]).astype(F32)
    columns[CLOSING] = (labels == labels[tokens - 1]).astype(F32)
    table = jnp.stack(columns, axis=1)
    at = jnp.arange(tokens)
    visible = (at[:, None] >= at[None, :]) & (labels[:, None] == labels[None, :])
    hide = jnp.where(visible, 0.0, HIDE).astype(F32)

    pairs = lax.axis_size("tp")
    column = jnp.arange(wide + LANES)
    shared = (column >= inner) & (column < wide)
    owner = (column - inner) * pairs // (2 * state)
    mine = (~shared | (owner == lax.axis_index("tp"))).astype(BF16)

    residual = hidden_in[0].astype(F32)
    residuals, records, layer_params = ([], [], [])
    for l in range(layer_count):
        taps = jnp.pad(flat[l, b:c].reshape(lags + 1, wide), ((0, 7 - lags), (0, 0)))
        params = (flat[l, :a].reshape(-1), taps, flat[l, c:], flat[l, a:b].reshape(-1), dims)
        residuals.append(residual)
        residual, saved = layer_forward(residual, gathered[l], params, table, hide)
        records.append(saved)
        layer_params.append(params)
    hidden_out = residual.astype(BF16)[None]

    upstream = cotangent[0].astype(F32)
    shards, smalls = ([None] * layer_count, [None] * layer_count)
    for l in reversed(range(layer_count)):
        upstream, shards[l], smalls[l] = layer_backward(
            upstream, residuals[l], records[l], gathered[l], layer_params[l], table, hide, mine, l > 0
        )

    cat = jnp.stack(shards, axis=0)
    grad_in = cat[:, :, : 2 * inner].reshape(in_proj.shape)
    grad_state = cat[:, :, 2 * inner : 2 * inner + 2 * state]
    grad_step = cat[:, :, 2 * inner + 2 * state : 2 * inner + 2 * state + head_count]
    grad_out = cat[:, :, -inner:]

    small = exchanged_sum(jnp.stack(smalls, axis=0))
    first_layer = lax.axis_index("fsdp") * per_shard
    small = lax.dynamic_slice_in_dim(small, first_layer, per_shard, 0)
    d = a + (lags + 1) * wide // LANES
    taps_out = small[:, a:d].reshape(per_shard, lags + 1, wide)
    heads_out = small[:, d : d + 3, :head_count]
    return (
        hidden_out,
        upstream[None],
        small[:, :a].reshape(per_shard, model),
        grad_in,
        grad_step,
        grad_state,
        grad_out,
        taps_out[:, :lags, :inner],
        taps_out[:, lags, :inner],
        taps_out[:, :lags, inner:],
        taps_out[:, lags, inner:],
        heads_out[:, BIAS],
        heads_out[:, DECAY],
        heads_out[:, SKIP],
        small[:, d + 3 :].reshape(per_shard, inner),
    )


def solution(mesh):
    wide, thin = (P("fsdp", "ctx", None), P("fsdp", "tp"))
    weights = (
        P(None, ROWS, None, "tp"),
        P(None, ROWS, "tp"),
        P(None, ROWS, None),
        P(None, ROWS, "tp"),
    )
    small = (
        P("fsdp", None, "tp"),
        thin,
        P("fsdp", None, None),
        P("fsdp", None),
        thin,
        thin,
        thin,
        thin,
    )
    return jax.shard_map(
        on_device,
        mesh=mesh,
        in_specs=(wide, P("fsdp", "ctx"), wide, P("fsdp", None)) + weights + small,
        out_specs=(wide, wide, P("fsdp", None)) + weights + small,
        check_vma=False,
    )
```
